32 devices in a mesh: expert: 16 (over z, y, x), replica: 2 (over core).
Axes of the slice: x: 2, y: 2, z: 4, core: 2. Of those that a mesh axis runs over, the one named last changes fastest.
Arguments:
- tokens: bfloat16 [4096, 2048], P(('expert', 'replica')), may hold values from -6 to 6
- routing: int32 [4096, 8], P(('expert', 'replica')), may hold values from 0 to 31, all different within a row; in each aligned block of 128 rows (0 to 127, 128 to 255, ...) at most 64 rows name the same one
- gate_error: bfloat16 [32, 384, 2048], P('expert'), may hold values from -6 to 6
Outputs:
- calibrated: float32 [32, 384, 2048], P('expert', None, 'replica')
The draws below stay inside these ranges and needn't reach their ends.
Inputs may be any that keep to these rules, and one draw needn't show every extreme that they name: `routing`: each row names 8 different experts; every expert is named by some row; within the 128 rows of one device no expert is named more than 64 times, and some expert reaches 64.
All inputs are finite; a program needn't handle non-finite values.
Results may differ from the reference program's by a relative error of at most 0.0003.
Values may be sent and summed in bfloat16 or wider, within the bound.
No kernel may reach another device: no remote copies, remote signals or barrier semaphores. Data moves between devices by JAX's collectives and lax.ppermute only.
A program may use at most 128 MiB of HBM per device.

```python
import math
import jax
import jax.numpy as jnp
import numpy as np
from jax import lax

D = 2048
FF = 384
TOP = 8
TOK_DEV = 128
EXPERTS = 32
TOKENS = 4096
CAP = 64
DEVICES = 32


def steps_of(stream_key, dims, split, least, high):
    gain, own = 1.0, jax.random.fold_in(stream_key, 6)
    for position, blocks in split:
        draws = jnp.exp(jax.random.uniform(jax.random.fold_in(own, position), (blocks,), jnp.float32, least / len(split), high / len(split)))
        gain = gain * jnp.repeat(draws, dims[position] // blocks).reshape([-1 if axis == position else 1 for axis in range(len(dims))])
    return gain


def routed_block(key, own, number, rows, amount, top, bound, slope):
    sequence = jax.random.permutation(key, amount)
    packed, usual = portions_of(amount, rows * top, bound, slope, True), portions_of(amount, rows * top, bound, slope, False)
    places = jnp.arange(amount)

    def named(lengths, turn):
        used = int((lengths > 0).sum())
        fixed = max(1, used // 4)
        moved = fixed + (places - fixed + turn * (used - fixed)) % max(1, amount - fixed)
        return jnp.zeros((amount,), jnp.int32).at[sequence[jnp.where(places < fixed, places, moved)]].set(jnp.asarray(lengths, jnp.int32))

    lengths = jnp.where(number % 4 == 0, named(packed, number // 4), named(usual, number - number // 4 - 1))
    mixed = jax.random.permutation(jax.random.fold_in(own, 3), amount)
    source_of, receiver = mixed[0:amount // 2 * 2:2], mixed[1:amount // 2 * 2:2]
    slack = jnp.minimum(lengths[source_of] - 1, bound - lengths[receiver]) // 2
    slack = jnp.where((source_of == sequence[0]) | (receiver == sequence[0]) | (lengths[receiver] == 0), 0, jnp.maximum(slack, 0))
    moved = jax.random.randint(jax.random.fold_in(own, 4), (amount // 2,), 0, 1 << 20) % (slack + 1)
    lengths = lengths.at[source_of].add(-moved).at[receiver].add(moved)
    labels = jnp.searchsorted(jnp.cumsum(lengths), jnp.arange(rows * top), side="right").astype(jnp.int32)
    grid = labels.reshape(top, rows).T
    grid = grid[jax.random.permutation(jax.random.fold_in(own, 1), rows)]
    turn = jax.random.randint(jax.random.fold_in(own, 2), (rows, 1), 0, top)
    return jnp.take_along_axis(grid, (jnp.arange(top)[None, :] + turn) % top, axis=1)


def portions_of(amount, total, most, slope, full):
    loads = [(1 << 20) // math.isqrt(standing ** slope) + 1 for standing in range(1, amount + 1)]
    largest = most if full else min(most, max(-(-total // amount), total * loads[0] // sum(loads)))
    least = 1 if total - largest >= amount - 1 else 0
    holding, spare = [largest] + [least] * (amount - 1), total - largest - least * (amount - 1)
    while spare > 0:
        movable = [i for i in range(1, amount) if holding[i] < largest] or [i for i in range(1, amount) if holding[i] < most]
        pool, left = sum([loads[i] for i in movable]), spare
        for i in movable:
            extra = min(most - holding[i], max(1, left * loads[i] // pool), spare)
            holding[i] = holding[i] + extra
            spare = spare - extra
    return np.array(holding)


def scatter_about(stream_key, extent, spread, bound, pieces=(), kind=jnp.bfloat16):
    drawn = jax.random.normal(stream_key, extent, jnp.float32) * spread
    if len(pieces) > 0:
        drawn = steps_of(stream_key, extent, pieces, -0.22, 0.18) * drawn
    return jnp.clip(drawn, min=-bound, max=bound).astype(kind)


def setup_inputs(seed: int = 0) -> dict:
    splits = jax.random.split(jax.random.key(seed), 4)
    tokens = scatter_about(splits[0], (TOKENS, D), 1.0, 6.0, ((0, 32),))
    routing_keys = jax.random.split(jax.random.fold_in(splits[1], 1), TOKENS // TOK_DEV)
    routing_turns = jax.random.permutation(jax.random.fold_in(splits[1], 3), TOKENS // TOK_DEV)
    routing = jax.vmap(lambda own, number: routed_block(jax.random.fold_in(splits[1], 2), own, number, TOK_DEV, EXPERTS, TOP, CAP, 2))(routing_keys, routing_turns).reshape((TOKENS, TOP))
    gate_error = scatter_about(splits[2], (EXPERTS, FF, D), 1.0, 6.0, ((0, 16),))
    return {"tokens": tokens, "routing": routing, "gate_error": gate_error}


def block_slots(flat_routes):
    onehot = (flat_routes[:, None] == jnp.arange(EXPERTS, dtype=jnp.int32)[None, :]).astype(jnp.int32)
    earlier = jnp.cumsum(onehot, axis=0) - onehot
    rank_seen = jnp.sum(earlier * onehot, axis=1)
    return (flat_routes * CAP + rank_seen).astype(jnp.int32)


def reference(tokens, routing, gate_error):
    blocks = routing.reshape(DEVICES, TOK_DEV * TOP)
    slot_index = jax.vmap(block_slots)(blocks)
    row_ids = (jnp.arange(DEVICES, dtype=jnp.int32)[:, None] * TOK_DEV
               + (jnp.arange(TOK_DEV * TOP, dtype=jnp.int32) // TOP)[None, :]).astype(jnp.int32)
    table = jnp.full((DEVICES, EXPERTS * CAP), -1, dtype=jnp.int32)
    table = table.at[jnp.arange(DEVICES, dtype=jnp.int32)[:, None], slot_index].set(row_ids)
    table = table.reshape(DEVICES, EXPERTS, CAP).transpose(1, 0, 2).reshape(EXPERTS, DEVICES * CAP)

    def one_expert(item):
        row_list, error_rows = item
        valid = row_list >= 0
        picked = jnp.take(tokens, jnp.maximum(row_list, 0), axis=0).astype(jnp.float32)
        picked = picked * valid[:, None].astype(jnp.float32)
        count = jnp.sum(valid.astype(jnp.float32))
        hessian = jnp.dot(picked.T, picked, precision=lax.Precision.HIGHEST) / count
        return jnp.dot(error_rows.astype(jnp.float32), hessian, precision=lax.Precision.HIGHEST)

    return lax.map(one_expert, (table, gate_error))
```

```python
import functools

import jax
import jax.numpy as jnp
from jax import lax
from jax.experimental import pallas as pl
from jax.experimental.pallas import tpu as pltpu
from jax.sharding import PartitionSpec as P

AXES = ("expert", "replica")


def grid_sides(chips):
    side = 1 << (chips.bit_length() - 1) // 3
    return chips // (side * side), side


def accumulate(units, first, last, idx_ref, mask_ref, err_ref, *refs):
    refs = list(refs)
    acc_ref = None if first else refs.pop(0)
    parts, (out_ref, buf, sems) = refs[: 2 * units], refs[2 * units :]
    experts, _, half = out_ref.shape
    rows = parts[0].shape[0]

    def fetch(g, h, src):
        return pltpu.make_async_copy(src, buf.at[g, pl.ds(h * rows, rows)], sems.at[g, h])

    for g in range(units):
        for h in range(2):
            fetch(g, h, parts[2 * g + h]).start()
    out_ref[...] = jnp.zeros_like(out_ref) if first else acc_ref[...]
    column = pl.multiple_of(idx_ref[2 * units] * half, half)

    def step(g, carry):
        for h in range(2):
            fetch(g, h, parts[h]).wait()
        block = buf[g]
        wanted = buf[g, :, pl.ds(column, half)]
        twice = jnp.concatenate([wanted, wanted], 0)
        masks = [mask_ref[idx_ref[2 * g + h]] for h in range(2)]
        for e in range(experts):
            scores = lax.dot_general(
                err_ref[e], block, (((1,), (1,)), ((), ())), preferred_element_type=jnp.float32
            )
            own = jnp.concatenate([m[:, e * rows : (e + 1) * rows] for m in masks], 1)
            scores = scores * own
            high = scores.astype(jnp.bfloat16)
            low = (scores - high.astype(jnp.float32)).astype(jnp.bfloat16)
            out_ref[e] += jnp.dot(
                jnp.concatenate([high, low], 1), twice, preferred_element_type=jnp.float32
            )
        return carry

    lax.fori_loop(0, units, step, 0)
    if last:
        for e in range(experts):
            count = jnp.sum(mask_ref[:, :, e * rows : (e + 1) * rows])
            out_ref[e] = out_ref[e] / count


def chunk_call(acc, pairs, index, masks, errors, last):
    units = len(pairs)
    first = acc is None
    rows, width = pairs[0][0].shape
    experts, outer, _ = errors.shape
    half = width // 2
    parts = [part for pair in pairs for part in pair]
    vmem = pl.BlockSpec(memory_space=pltpu.VMEM)
    out = jax.ShapeDtypeStruct((experts, outer, half), jnp.float32)
    heads = [index, masks, errors] + ([] if first else [acc])
    specs = [pl.BlockSpec(memory_space=pltpu.SMEM)] + [vmem] * (len(heads) - 1)
    work = 2 * experts * outer * 2 * rows * units * (width + 2 * half)
    return pl.pallas_call(
        functools.partial(accumulate, units, first, last),
        out_shape=out,
        in_specs=specs + [pl.BlockSpec(memory_space=pl.ANY)] * len(parts),
        out_specs=vmem,
        scratch_shapes=[
            pltpu.VMEM((units, 2 * rows, width), jnp.bfloat16),
            pltpu.SemaphoreType.DMA((units, 2)),
        ],
        compiler_params=pltpu.CompilerParams(vmem_limit_bytes=28 << 20),
        cost_estimate=pl.CostEstimate(flops=work, bytes_accessed=16 << 20, transcendentals=0),
    )(*heads, *parts)


def local(tokens, routing, gate_error):
    chips = lax.axis_size("expert")
    cores = lax.axis_size("replica")
    deep, side = grid_sides(chips)
    rows, width = tokens.shape
    experts = gate_error.shape[0] * chips
    chip, core = lax.axis_index("expert"), lax.axis_index("replica")

    def place(z, y, x):
        return (z % deep * side + y % side) * side + x % side

    def split(c):
        return c // (side * side), c // side % side, c % side

    def moves(dz, first, second):
        pairs = []
        for c in range(chips):
            z, y, x = split(c)
            for r in range(cores):
                dx, dy = (first, second) if r == 0 else (second, first)
                pairs.append((c * cores + r, place(z + dz, y + dy, x + dx) * cores + r))
        return pairs

    up, one, two = moves(1, 0, 0), moves(0, 1, 0), moves(0, 0, 1)
    swap = [(d, d ^ 1) for d in range(chips * cores)]
    send = lambda shard, pairs: lax.ppermute(shard, AXES, pairs)

    member = (routing[None] == jnp.arange(experts, dtype=jnp.int32)[:, None, None]).any(-1)
    member = member.astype(jnp.float32).reshape(chips, 1, 1, -1)
    member = jnp.broadcast_to(member, (chips, cores, 1, member.shape[-1]))
    masks = lax.all_to_all(
        member.reshape(chips * cores, 1, -1), AXES, split_axis=0, concat_axis=0, tiled=True
    )

    def source(j, a, b, r):
        z, y, x = split(chip)
        dx, dy = jnp.where(r == 0, a, b), jnp.where(r == 0, b, a)
        return place(z - j + deep, y - dy + side, x - dx + side) * cores + r

    units = []
    level = tokens
    for j in range(deep):
        if j:
            level = send(level, up)
        line = [level]
        for a in range(1, side):
            line.append(send(line[-1], one))
        for a, part in enumerate(line):
            units.append((part, (j, a, 0)))
        for b in range(1, side):
            line = [send(part, two) for part in line]
            for a, part in enumerate(line):
                units.append((part, (j, a, b)))

    size = min(side * side, 4)
    groups = [units[i : i + size] for i in range(0, len(units), size)]
    final = groups.pop()
    groups += [final[:-1], final[-1:]]
    acc = None
    for number, group in enumerate(groups):
        pairs = [(part, send(part, swap)) for part, _ in group]
        index = [source(*where, r) for _, where in group for r in (core, 1 - core)] + [core]
        index = jnp.stack(index).astype(jnp.int32)
        acc = chunk_call(acc, pairs, index, masks, gate_error, number == len(groups) - 1)
    return acc


def solution(mesh):
    in_specs = (
        P(("expert", "replica"), None),
        P(("expert", "replica"), None),
        P("expert", None, None),
    )
    out_specs = P("expert", None, "replica")
    return jax.shard_map(local, mesh=mesh, in_specs=in_specs, out_specs=out_specs, check_vma=False)
```

```python
import functools

import jax
import jax.numpy as jnp
from jax import lax
from jax.experimental import pallas as pl
from jax.experimental.pallas import tpu as pltpu
from jax.sharding import PartitionSpec as P

AXES = ("expert", "replica")
VMEM_LIMIT = 24 << 20
GROUP = 4


def grid_sides(chips):
    side = 1 << (chips.bit_length() - 1) // 3
    return chips // (side * side), side


def finish(places, parts, source, rank_ref, err_ref, acc_refs, out_ref, done_ref, sems):
    experts, outer, half = done_ref.shape
    rows = rank_ref.shape[2] // experts
    width = err_ref.shape[2]
    tile = min(512, half)
    core = lax.axis_index("replica")
    pieces = [piece for unit in parts for piece in unit]
    ranks = [rank_ref[source(*where)] for where in places]
    block = jnp.concatenate([piece[...] for piece in pieces], 0)
    scores = lax.dot_general(
        err_ref[...].reshape(experts * outer, width),
        block,
        (((1,), (1,)), ((), ())),
        preferred_element_type=jnp.float32,
    )
    tiles = half // tile

    def leave(e, t):
        lanes = pl.ds(t * tile, tile)
        return pltpu.make_async_copy(
            done_ref.at[e, :, lanes], out_ref.at[e, :, lanes], sems.at[e, t]
        )

    for e in range(experts):
        row = jnp.concatenate([r[:, e * rows : (e + 1) * rows] for r in ranks], 1)
        mine = jnp.where(row >= 0, scores[e * outer : (e + 1) * outer], 0.0)
        high = mine.astype(jnp.bfloat16)
        low = (mine - high.astype(jnp.float32)).astype(jnp.bfloat16)
        left = jnp.concatenate([high, low], 0)
        named = rank_ref[:, :, e * rows : (e + 1) * rows] >= 0
        scale = 1.0 / jnp.sum(named.astype(jnp.float32))
        for t in range(tiles):
            lanes = pl.ds(t * tile, tile)
            source_lanes = pl.ds(pl.multiple_of(core * half + t * tile, tile), tile)
            right = jnp.concatenate([piece[:, source_lanes] for piece in pieces], 0)
            both = jnp.dot(left, right, preferred_element_type=jnp.float32)
            total = both[:outer] + both[outer:]
            for acc_ref in acc_refs:
                total = total + acc_ref[e, :, lanes]
            done_ref[e, :, lanes] = total * scale
            leave(e, t).start()
    for e in range(experts):
        for t in range(tiles):
            leave(e, t).wait()


def accumulate(places, splits, cap, sums, last, rank_ref, err_ref, *refs):
    units = len(places)
    acc_refs, refs = refs[:sums], list(refs[sums:])
    parts = [[refs.pop(0) for _ in range(pieces)] for pieces in splits]
    scratch = refs[-2:] if last else refs[-1:]
    out_refs, packed = refs[: -len(scratch)], scratch[0]
    experts, outer, half = out_refs[0].shape
    rows = rank_ref.shape[2] // experts
    width = parts[0][0].shape[1]
    tile = min(512, half)
    chip, core = lax.axis_index("expert"), lax.axis_index("replica")
    cores = lax.axis_size("replica")
    deep, side = grid_sides(lax.axis_size("expert"))

    def source(j, a, b, flip):
        r = 1 - core if flip else core
        dx, dy = jnp.where(r == 0, a, b), jnp.where(r == 0, b, a)
        x = (chip - dx) & (side - 1)
        y = (chip // side - dy) & (side - 1)
        z = (chip // (side * side) - j) & (deep - 1)
        return ((z * side + y) * side + x) * cores + r

    if last:
        finish(places, parts, source, rank_ref, err_ref, acc_refs, *out_refs, *scratch)
        return

    for begin in range(0, units, 2):
        chosen_units = range(begin, min(begin + 2, units))
        picked = len(chosen_units) * cap
        ranks = [rank_ref[source(*places[u])] for u in chosen_units]
        ranks = [jnp.where(r < 0, r, r + n * cap) for n, r in enumerate(ranks)]
        slot = lax.broadcasted_iota(jnp.int32, (picked, len(ranks) * rows), 0)
        slot = slot.astype(jnp.float32)
        pick = []
        for e in range(experts):
            row = jnp.concatenate([r[:, e * rows : (e + 1) * rows] for r in ranks], 1)
            pick.append((slot == row).astype(jnp.float32).astype(jnp.bfloat16))
        pick = jnp.concatenate(pick, 0)
        pieces = [piece for u in chosen_units for piece in parts[u]]

        def choose(t, carry):
            lanes = pl.ds(pl.multiple_of(t * tile, tile), tile)
            block = jnp.concatenate([piece[:, lanes] for piece in pieces], 0)
            chosen = jnp.dot(pick, block, preferred_element_type=jnp.float32)
            chosen = chosen.astype(jnp.bfloat16)
            for e in range(experts):
                packed[e, begin * cap : begin * cap + picked, lanes] = chosen[
                    e * picked : (e + 1) * picked
                ]
            return carry

        lax.fori_loop(0, width // tile, choose, 0)

    lefts = []
    for e in range(experts):
        scores = lax.dot_general(
            err_ref[e], packed[e], (((1,), (1,)), ((), ())), preferred_element_type=jnp.float32
        )
        high = scores.astype(jnp.bfloat16)
        low = (scores - high.astype(jnp.float32)).astype(jnp.bfloat16)
        lefts.append(jnp.concatenate([high, low], 0))

    for w, out_ref in enumerate(out_refs):
        start = (1 - core if w else core) * half
        for e in range(experts):

            def spread(t, carry):
                lanes = pl.ds(pl.multiple_of(t * tile, tile), tile)
                right = packed[e, :, pl.ds(pl.multiple_of(start + t * tile, tile), tile)]
                both = jnp.dot(lefts[e], right, preferred_element_type=jnp.float32)
                total = both[:outer] + both[outer:]
                for acc_ref in acc_refs[w :: len(out_refs)]:
                    total = total + acc_ref[e, :, lanes]
                out_ref[e, :, lanes] = total
                return carry

            lax.fori_loop(0, half // tile, spread, 0)


def chunk_call(acc, units, ranks, errors, cap, outs, last):
    parts = [piece for unit, _ in units for piece in unit]
    places = [where for _, where in units]
    splits = [len(unit) for unit, _ in units]
    rows, width = ranks.shape[2] // errors.shape[0], parts[0].shape[1]
    experts, outer, _ = errors.shape
    half = width // 2
    vmem = pl.BlockSpec(memory_space=pltpu.VMEM)
    operands = [ranks, errors, *acc, *parts]
    depth = len(units) * cap
    scratch = [pltpu.VMEM((experts, depth, width), jnp.bfloat16)]
    if last:
        sems = pltpu.SemaphoreType.DMA((experts, half // min(512, half)))
        scratch = [pltpu.VMEM((experts, outer, half), jnp.float32), sems]
    work = 2 * experts * depth * (2 * rows * width + outer * (width + 2 * outs * half))
    return pl.pallas_call(
        functools.partial(accumulate, places, splits, cap, len(acc), last),
        out_shape=[jax.ShapeDtypeStruct((experts, outer, half), jnp.float32)] * outs,
        in_specs=[vmem] * len(operands),
        out_specs=[pl.BlockSpec(memory_space=pl.ANY) if last else vmem] * outs,
        scratch_shapes=scratch,
        compiler_params=pltpu.CompilerParams(vmem_limit_bytes=VMEM_LIMIT),
        cost_estimate=pl.CostEstimate(flops=work, bytes_accessed=8 << 20, transcendentals=0),
    )(*operands)


def local(tokens, routing, gate_error):
    chips = lax.axis_size("expert")
    cores = lax.axis_size("replica")
    deep, side = grid_sides(chips)
    rows, _ = tokens.shape
    experts = gate_error.shape[0] * chips
    cap = 2 * rows * routing.shape[1] // experts

    def place(z, y, x):
        return (z % deep * side + y % side) * side + x % side

    def split(c):
        return c // (side * side), c // side % side, c % side

    def moves(dz, first, second):
        pairs = []
        for c in range(chips):
            z, y, x = split(c)
            for r in range(cores):
                dx, dy = (first, second) if r == 0 else (second, first)
                pairs.append((c * cores + r, place(z + dz, y + dy, x + dx) * cores + r))
        return pairs

    up, down, one, two = moves(1, 0, 0), moves(deep - 1, 0, 0), moves(0, 1, 0), moves(0, 0, 1)
    swap = [(d, d ^ 1) for d in range(chips * cores)]

    def send(shard, pairs):
        return lax.ppermute(shard, AXES, pairs)

    member = (routing[None] == jnp.arange(experts, dtype=jnp.int32)[:, None, None]).any(-1)
    ahead = jnp.dot(
        member.astype(jnp.bfloat16),
        jnp.triu(jnp.ones((rows, rows), jnp.bfloat16)),
        preferred_element_type=jnp.float32,
    )
    ranks = jnp.where(member, ahead - 1, -1).reshape(chips, 1, 1, -1)
    ranks = jnp.broadcast_to(ranks, (chips, cores, 1, ranks.shape[-1]))
    ranks = lax.all_to_all(
        ranks.reshape(chips * cores, 1, -1), AXES, split_axis=0, concat_axis=0, tiled=True
    )

    levels = []
    level = tokens
    corners = {}
    for j in range(deep):
        if j:
            level = send(level, up)
        line = [level]
        for _ in range(1, side):
            line.append(send(line[-1], one))
        units = [((part,), (j, a, 0, False)) for a, part in enumerate(line)]
        for a, part in enumerate(line):
            for b in range(1, side):
                if a and j in (1, deep - 1):
                    part = send(corners[a, b], up if j == 1 else down)
                else:
                    part = send(part, two)
                if a and j == 0:
                    corners[a, b] = part
                units.append(((part,), (j, a, b, False)))
        levels.append(units)

    def paired(units):
        full = []
        for unit, where in units:
            full.append((unit, where))
            other = tuple(send(piece, swap) for piece in unit)
            full.append((other, (*where[:3], True)))
        return full

    acc = []
    final = levels.pop()
    held = [levels[1].pop(), levels[-1].pop()]
    early = [unit for units in levels for unit in units] + [final.pop(0)]
    if side == 2:
        early[6], early[7] = early[7], early[6]
    bounds = [0, *range(side * side - 1, len(early), GROUP), len(early)]
    for begin, end in zip(bounds, bounds[1:]):
        acc = chunk_call(acc, early[begin:end], ranks, gate_error, cap, 2, False)
    kept, given = acc
    taken = send(given, swap)
    groups = [held, *[final[i : i + 2] for i in range(0, len(final) - 1, 2)], final[-1:]]
    for number, units in enumerate(groups):
        last = number == len(groups) - 1
        acc = [kept, taken] if last else [kept]
        units = paired(units)
        (kept,) = chunk_call(acc, units, ranks, gate_error, cap, 1, last)
    return kept


def solution(mesh):
    in_specs = (
        P(("expert", "replica"), None),
        P(("expert", "replica"), None),
        P("expert", None, None),
    )
    out_specs = P("expert", None, "replica")

    return jax.shard_map(local, mesh=mesh, in_specs=in_specs, out_specs=out_specs, check_vma=False)
```
